512 devices in a mesh: tile: 128 (over x, z, y_lo), spec: 4 (over y_hi, core).
Axes of the slice: x: 4, y: 8 (y_hi: 2, y_lo: 4; y = y_hi * 4 + y_lo), z: 8, core: 2. Of those that a mesh axis runs over, the one named last changes fastest.
Arguments:
- adjoint: float32 [128, 8, 512, 128], P('spec', None, 'tile'), may hold values from -6 to 6
- section_first: bfloat16 [128, 8, 128, 128], P('tile'), may hold values from -1 to 2
- section_second: bfloat16 [128, 8, 128, 128], P('tile'), may hold values from -1 to 2
- jacobian: bfloat16 [128, 8, 128, 128], P('tile'), may hold values from -0.5 to 0.5
- pattern: int32 [128, 8, 2, 2], P('tile'), may hold values 0 or 1
- counts: int32 [128, 8], P('tile'), may hold values from 1 to 512, as said below
- courant: float32 [8, 512, 128], P(None, 'tile'), may hold values from -0.45 to 0.45
- seam_codes: int32 [128, 2], P('tile'), may hold values from 0 to 1, as said below
Outputs:
- adjoint_out: float32 [128, 8, 512, 128], P('spec', None, 'tile')
The draws below stay inside these ranges and needn't reach their ends.
Inputs may be any that keep to these rules, and one draw needn't show every extreme that they name: The active cells of tile t and level l are the first counts[t, l] of its 4 x 128 cells in row-major order. `seam_codes`: column 0 of tile t is the code of the seam between tile t and tile t + 1, column 1 that of the seam between tile t - 1 and tile t (cyclically); a 1 means that the seam reverses the order of cells along it. `pattern`: 1 where a block is present.
All inputs are finite; a program needn't handle non-finite values.
Results may differ from the reference program's by a relative error of at most 0.004.
Values may be sent and summed in bfloat16 or wider, within the bound.
No kernel may reach another device: no remote copies, remote signals or barrier semaphores. Data moves between devices by JAX's collectives and lax.ppermute only.
A program may use at most 64 MiB of HBM per device.

```python
import math
import jax
import jax.numpy as jnp

SPECIES = 128
BLK = 64
LEV = 8
CX = 4
CY = 128
NSUB = 4
TILES = 128
NX = 512
NBLK = 2


def make_factor(key, salt, uniform_law):
    sub_key = jax.random.fold_in(key, salt)
    full_shape = (TILES, LEV, SPECIES, SPECIES)
    if uniform_law:
        noise_draw = jax.random.uniform(sub_key, full_shape, jnp.float32, -1.7320508, 1.7320508)
    else:
        noise_draw = jax.random.normal(sub_key, full_shape, jnp.float32)
    identity = jnp.eye(SPECIES, dtype=jnp.float32)
    return (identity[None, None] + 0.5 * noise_draw / math.sqrt(SPECIES)).astype(jnp.bfloat16)


def draw_section_first(key, part):
    return make_factor(key, 11, False)


def draw_section_second(key, part):
    return make_factor(key, 13, False)


def draw_counts(key, part):
    total_slots = TILES * LEV
    count_draw = jax.random.randint(jax.random.fold_in(key, 31), (total_slots,), 1, CX * CY + 1)
    first_slot = jax.random.randint(jax.random.fold_in(key, 37), (), 0, total_slots)
    offset_slot = jax.random.randint(jax.random.fold_in(key, 41), (), 0, total_slots - 1)
    second_slot = (first_slot + 1 + offset_slot) % total_slots
    count_draw = count_draw.at[second_slot].set(1)
    count_draw = count_draw.at[first_slot].set(CX * CY)
    return count_draw.reshape(TILES, LEV).astype(jnp.int32)


def draw_seam_codes(key, part):
    seam_flags = jax.random.randint(jax.random.fold_in(key, 23), (TILES,), 0, 2)
    return jnp.stack([seam_flags, jnp.roll(seam_flags, 1)], axis=1).astype(jnp.int32)


def touch_ends(array, stream_key, low, largest):
    longest = array.shape.index(max(array.shape))
    spots = []
    for shift in (0, 1):
        where = [jax.random.randint(jax.random.fold_in(stream_key, axis), (), 0, length) for axis, length in enumerate(array.shape)]
        where[longest] = (where[longest] + shift) % array.shape[longest]
        spots.append(tuple(where))
    return array.at[spots[0]].set(low).at[spots[1]].set(largest)


def level_of(stream_key, extent, shards, smallest, largest):
    level = 1.0
    for position, blocks in shards:
        heights = jax.random.uniform(jax.random.fold_in(jax.random.fold_in(stream_key, 6), position), (blocks,), jnp.float32, smallest / len(shards), largest / len(shards))
        level = level * jnp.repeat(jnp.exp(heights), extent[position] // blocks).reshape((-1,) + (1,) * (len(extent) - 1 - position))
    return level


def bell_draw(rng, dims, spread, most, shards=(), kind=jnp.bfloat16):
    result = jax.random.normal(rng, dims, jnp.float32) * spread
    if len(shards) > 0:
        result = level_of(rng, dims, shards, -0.22, 0.18) * result
    return jnp.clip(result, min=-most, max=most).astype(kind)


def setup_inputs(seed: int = 0) -> dict:
    key_of = jax.random.split(jax.random.key(seed), 9)
    adjoint = bell_draw(key_of[0], (SPECIES, LEV, NX, CY), 1.0, 6.0, ((0, 4), (2, 128)), jnp.float32)
    section_first = draw_section_first(jax.random.fold_in(key_of[8], 71), 0)
    section_second = draw_section_second(jax.random.fold_in(key_of[8], 71), 0)
    jacobian = bell_draw(key_of[3], (TILES, LEV, SPECIES, SPECIES), SPECIES ** -0.5, 0.5, ((0, 128),))
    pattern = touch_ends((jax.random.randint(key_of[4], (TILES, LEV, NBLK, NBLK), 0, 4) < 3).astype(jnp.int32), jax.random.fold_in(key_of[4], 1), 0, 1)
    counts = draw_counts(jax.random.fold_in(key_of[8], 71), 0)
    courant = jnp.clip(jax.random.uniform(key_of[6], (LEV, NX, CY), jnp.float32, -0.45, 0.45) * level_of(key_of[6], (LEV, NX, CY), ((1, 128),), -0.4, 0.0), -0.45, 0.45)
    seam_codes = draw_seam_codes(jax.random.fold_in(key_of[8], 71), 0)
    return {"adjoint": adjoint, "section_first": section_first, "section_second": section_second, "jacobian": jacobian, "pattern": pattern, "counts": counts, "courant": courant, "seam_codes": seam_codes}


section_weights = (0.4, 0.3, 0.2, 0.1)
coupling = 0.5


def transposed(matrix, field_tiles):
    return jnp.einsum("tlsp,sltc->pltc", matrix.astype(jnp.float32), field_tiles.astype(jnp.float32))


def reference(adjoint, section_first, section_second, jacobian, pattern, counts, courant, seam_codes):
    cell_count = CX * CY
    field_tiles = adjoint.reshape(SPECIES, LEV, TILES, cell_count)
    rounded = field_tiles.astype(jnp.bfloat16)
    present = jnp.repeat(jnp.repeat(pattern, BLK, axis=2), BLK, axis=3) == 1
    jac_used = jnp.where(present, jacobian, jnp.zeros_like(jacobian))
    start_wide = rounded.astype(jnp.float32)
    first_y = transposed(section_first, rounded).astype(jnp.bfloat16)
    section_u = transposed(section_second, first_y).astype(jnp.bfloat16)
    running_sum = None
    for section in range(4):
        coupled = transposed(jac_used, section_u)
        if section == 0:
            running_sum = section_weights[0] * coupled
        else:
            running_sum = running_sum + section_weights[section] * coupled
        if section < 3:
            mixed_term = (start_wide + coupling * coupled).astype(jnp.bfloat16)
            first_y = transposed(section_first, mixed_term).astype(jnp.bfloat16)
            section_u = transposed(section_second, first_y).astype(jnp.bfloat16)
    chemistry = running_sum.astype(jnp.bfloat16).astype(jnp.float32)
    cell_index = jnp.arange(cell_count, dtype=jnp.int32)
    active_mask = cell_index[None, None, :] < jnp.transpose(counts)[:, :, None]
    adjoint_state = field_tiles + jnp.where(active_mask[None], chemistry, jnp.zeros_like(chemistry))
    adjoint_state = adjoint_state.reshape(SPECIES, LEV, NX, CY)
    row_index = jnp.arange(NX, dtype=jnp.int32)
    owner_tile = row_index // CX
    flip_up = (row_index % CX == CX - 1) & (seam_codes[owner_tile, 0] == 1)
    flip_down = (row_index % CX == 0) & (seam_codes[owner_tile, 1] == 1)
    lower_faces = jnp.roll(courant, 1, axis=1)
    lower_faces = jnp.where(flip_down[None, :, None], lower_faces[..., ::-1], lower_faces)
    rising = jnp.maximum(courant, 0.0)
    falling = jnp.minimum(lower_faces, 0.0)
    for substep in range(NSUB):
        above_cells = jnp.roll(adjoint_state, -1, axis=2)
        above_cells = jnp.where(flip_up[None, None, :, None], above_cells[..., ::-1], above_cells)
        below_cells = jnp.roll(adjoint_state, 1, axis=2)
        below_cells = jnp.where(flip_down[None, None, :, None], below_cells[..., ::-1], below_cells)
        adjoint_state = adjoint_state + rising * (above_cells - adjoint_state) + falling * (adjoint_state - below_cells)
    return adjoint_state
```

```python
import functools

import jax
import jax.numpy as jnp
import numpy as np
from jax import lax
from jax.experimental import pallas as pl
from jax.experimental.pallas import tpu as pltpu
from jax.sharding import PartitionSpec as P

NSUB = 4
section_weights = (0.4, 0.3, 0.2, 0.1)
coupling = 0.5
AXES = ("tile", "spec")
RUN = 4

VMEM = pltpu.VMEM
SMEM = pltpu.SMEM


def whole(space):
    return pl.BlockSpec(memory_space=space)


def call(body, out_shape, in_specs, out_specs, scratch=(), cost=(0, 0), name=None):
    return pl.pallas_call(
        body,
        out_shape=out_shape,
        in_specs=in_specs,
        out_specs=out_specs,
        scratch_shapes=list(scratch),
        cost_estimate=pl.CostEstimate(flops=cost[0], bytes_accessed=cost[1], transcendentals=0),
        name=name,
    )


def partner_table(tiles, spec):
    rows = []
    partner = []
    for tile in range(tiles):
        for s in range(spec):
            core = s % 2
            half = s // 2
            up = (tile % 2 == 0) == (core == 0)
            step = 1 if up else -1
            other = (tile + step) % tiles
            wraps = not 0 <= tile % RUN + step < RUN
            other_half = half ^ 1 if wraps else half
            partner.append(other * spec + other_half * 2 + core)
            rows.append([core, half, other_half, int(up), s, 0, 0, 0])
    for source, target in enumerate(partner):
        assert partner[target] == source
    return np.array(rows, np.int32), list(enumerate(partner))


def start_body(adj_ref, start_ref, held, sems):
    levels, rows = adj_ref.shape[1], adj_ref.shape[2]
    copies = []
    for level in range(levels):
        for row in range(rows):
            q = level * rows + row
            copies.append(
                pltpu.make_async_copy(adj_ref.at[:, level, row, :], held.at[q], sems.at[level])
            )
            copies[-1].start()
    for level in range(levels):
        for row in range(rows):
            copies[level * rows + row].wait()
        part = pl.ds(level * rows, rows)
        start_ref[part] = held[part].astype(jnp.bfloat16)


def matrix_body(pattern_ref, table_ref, first_ref, second_ref, jac_ref, high_ref, low_ref, held):
    levels, size = first_ref.shape[1], first_ref.shape[2]
    block = size // 2
    w = section_weights
    ones = (w[0] + w[1] + w[2] + w[3], coupling * (w[1] + w[2] + w[3]))
    c2 = coupling * ones[1] - coupling * coupling * w[1]
    c3 = coupling**3 * w[3]
    lane = lax.broadcasted_iota(jnp.int32, (block, size), 1)
    row_id = lax.broadcasted_iota(jnp.int32, (size, size), 0)
    col_id = lax.broadcasted_iota(jnp.int32, (size, size), 1)
    diag = row_id == col_id

    def dot(a, b):
        return jnp.dot(a, b, preferred_element_type=jnp.float32)

    def used(level):
        parts = []
        for b in range(2):
            keep = jnp.where(lane < block, pattern_ref[0, level, b, 0], pattern_ref[0, level, b, 1])
            piece = jac_ref[0, level, pl.ds(b * block, block), :].astype(jnp.float32)
            parts.append(jnp.where(keep == 1, piece, 0.0).astype(jnp.bfloat16))
        return jnp.concatenate(parts, axis=0)

    for group in range(0, levels, 4):
        span = range(group, group + 4)
        t = [dot(second_ref[0, l], used(l)) for l in span]
        t_high = [x.astype(jnp.bfloat16) for x in t]
        t_low = [(x - h.astype(jnp.float32)).astype(jnp.bfloat16) for x, h in zip(t, t_high)]
        k = [
            dot(first_ref[0, l], h) + dot(first_ref[0, l], lo) for l, h, lo in zip(span, t_high, t_low)
        ]
        kb = [x.astype(jnp.bfloat16) for x in k]
        acc = [c3 * x + jnp.where(diag, c2, 0.0) for x in k]
        acc = [dot(a, x.astype(jnp.bfloat16)) + jnp.where(diag, ones[1], 0.0) for a, x in zip(kb, acc)]
        acc = [dot(a, x.astype(jnp.bfloat16)) for a, x in zip(kb, acc)]
        d = [
            x * ones[0] + dot(a, h.astype(jnp.bfloat16)) for x, a, h in zip(k, kb, acc)
        ]
        for i, l in enumerate(span):
            held[l] = d[i]
    own = pl.multiple_of(table_ref[0, 1] * block, block)
    far = pl.multiple_of((1 - table_ref[0, 1]) * block, block)
    for l in range(levels):
        ordered = jnp.concatenate([held[l, pl.ds(own, block), :], held[l, pl.ds(far, block), :]], axis=0)
        turned = ordered.T
        high = turned.astype(jnp.bfloat16)
        high_ref[l] = high
        low_ref[l] = (turned - high.astype(jnp.float32)).astype(jnp.bfloat16)


def fields(near_ref, far_ref, level, rows):
    return jnp.concatenate(
        [
            jnp.concatenate([near_ref[0, q], near_ref[1, q], far_ref[0, q], far_ref[1, q]], axis=0)
            for q in range(level * rows, level * rows + rows)
        ],
        axis=1,
    )


def rim_body(counts_ref, table_ref, near_ref, far_ref, high_ref, cour_ref, msg_ref):
    rows = cour_ref.shape[0]
    levels = high_ref.shape[0]
    cells = near_ref.shape[3]
    own = near_ref.shape[2]
    quads = levels * rows
    aim = pl.multiple_of(table_ref[0, 2] * 2 * own, 2 * own)
    near_aim = table_ref[0, 2] == table_ref[0, 1]
    lane = lax.broadcasted_iota(jnp.int32, (own, cells), 1)
    sections = (0, quads * own + 3 * quads)
    for level in range(levels):
        x = fields(near_ref, far_ref, level, rows)
        chem = jnp.dot(high_ref[level, pl.ds(aim, 2 * own), :], x, preferred_element_type=jnp.float32)
        for row in range(rows):
            q = level * rows + row
            active = lane < counts_ref[0, level] - row * cells
            for core in range(2):
                base = jnp.where(
                    near_aim,
                    near_ref[core, q].astype(jnp.float32),
                    far_ref[core, q].astype(jnp.float32),
                )
                term = chem[core * own : (core + 1) * own, row * cells : (row + 1) * cells]
                value = base + jnp.where(active, term, 0.0)
                msg_ref[pl.ds(sections[core] + q * own, own), :] = value.astype(jnp.bfloat16)
    cour = jnp.concatenate([cour_ref[row] for row in range(rows)], axis=0)
    first = quads * own
    for piece in range(3):
        part = cour.astype(jnp.bfloat16)
        msg_ref[pl.ds(first + piece * quads, quads), :] = part
        cour = cour - part.astype(jnp.float32)


def own_body(counts_ref, table_ref, adj_ref, near_ref, far_ref, high_ref, low_ref, after_ref, held, sems):
    levels, rows = adj_ref.shape[1], adj_ref.shape[2]
    own, cells = adj_ref.shape[0], adj_ref.shape[3]
    copies = []
    for level in range(levels):
        for row in range(rows):
            q = level * rows + row
            copies.append(
                pltpu.make_async_copy(adj_ref.at[:, level, row, :], held.at[q], sems.at[level])
            )
            copies[-1].start()
    mine = pl.multiple_of(table_ref[0, 4] * own, own)
    lane = lax.broadcasted_iota(jnp.int32, (own, cells), 1)
    for level in range(levels):
        x = fields(near_ref, far_ref, level, rows)
        both = jnp.concatenate(
            [high_ref[level, pl.ds(mine, own), :], low_ref[level, pl.ds(mine, own), :]], axis=0
        )
        chem = jnp.dot(both, x, preferred_element_type=jnp.float32)
        chem = chem[:own] + chem[own:]
        for row in range(rows):
            copies[level * rows + row].wait()
        for row in range(rows):
            q = level * rows + row
            active = lane < counts_ref[0, level] - row * cells
            term = chem[:, row * cells : (row + 1) * cells]
            after_ref[q] = held[q] + jnp.where(active, term, 0.0)


def taps(rise, fall, rows):
    table = []
    for i in range(rows, 2 * rows):
        weight = {i: None}
        for _ in range(NSUB):
            fresh = {}

            def add(j, value, fresh=fresh):
                fresh[j] = value if j not in fresh else fresh[j] + value

            for j, value in weight.items():
                keep = 1.0 - rise[j] + fall[j]
                add(j, keep if value is None else value * keep)
                add(j + 1, rise[j] if value is None else value * rise[j])
                add(j - 1, -fall[j] if value is None else -(value * fall[j]))
            weight = fresh
        table.append(weight)
    return table


def end_body(table_ref, codes_ref, after_ref, got_ref, handed_ref, cour_ref, out_ref, coef, built, sems):
    rows = cour_ref.shape[0]
    levels = cour_ref.shape[1]
    own, cells = after_ref.shape[1], after_ref.shape[2]
    quads = levels * rows
    body_rows = quads * own
    cour_rows = 3 * quads
    core = table_ref[0, 0]
    up = table_ref[0, 3] == 1
    got_at = core * (body_rows + cour_rows)
    handed_at = core * cour_rows
    handed_cour = (1 - core) * body_rows
    one = jnp.ones((cells, cells), jnp.float32)
    r = lax.broadcasted_iota(jnp.int32, (cells, cells), 0)
    c = lax.broadcasted_iota(jnp.int32, (cells, cells), 1)

    def turn(code):
        return jnp.where(jnp.where(code == 1, cells - 1 - c, c) == r, one, 0.0).astype(jnp.bfloat16)

    turn_up, turn_down = turn(codes_ref[0, 0]), turn(codes_ref[0, 1])

    def pair(got_row, handed_row, count):
        a = got_ref[pl.ds(pl.multiple_of(got_row, 32), count), :]
        b = handed_ref[1 - core, pl.ds(pl.multiple_of(handed_row, 32), count), :]
        a32, b32 = a.astype(jnp.float32), b.astype(jnp.float32)
        above = jnp.where(up, a32, b32).astype(jnp.bfloat16)
        below = jnp.where(up, b32, a32).astype(jnp.bfloat16)
        return (
            jnp.dot(above, turn_up, preferred_element_type=jnp.float32),
            jnp.dot(below, turn_down, preferred_element_type=jnp.float32),
        )

    pieces = pair(body_rows, handed_cour, cour_rows)
    above_cour, below_cour = [x[:quads] + x[quads : 2 * quads] + x[2 * quads :] for x in pieces]
    stack = [below_cour[i * levels : (i + 1) * levels] for i in range(rows)]
    stack += [cour_ref[i] for i in range(rows)]
    stack += [above_cour[i * levels : (i + 1) * levels] for i in range(rows)]
    rise = [jnp.maximum(x, 0.0) for x in stack]
    fall = [None] + [jnp.minimum(x, 0.0) for x in stack[:-1]]
    table = taps(rise, fall, rows)
    slot = {}
    for i, weight in enumerate(table):
        for j in sorted(weight):
            slot[i, j] = len(slot)
            coef[slot[i, j]] = weight[j]
    copies = []
    for level in range(levels):
        q = level * rows
        above, below = pair(got_at + q * own, handed_at + q * own, rows * own)
        stack = [below[i * own : (i + 1) * own] for i in range(rows)]
        stack += [after_ref[q + i] for i in range(rows)]
        stack += [above[i * own : (i + 1) * own] for i in range(rows)]
        for i in range(rows):
            total = None
            for j in sorted(table[i]):
                term = coef[slot[i, j], pl.ds(level, 1), :] * stack[j]
                total = term if total is None else total + term
            built[q + i] = total
        for i in range(rows):
            copies.append(
                pltpu.make_async_copy(built.at[q + i], out_ref.at[:, level, i, :], sems.at[level])
            )
            copies[-1].start()
    for copy in copies:
        copy.wait()


def shards(pairs, table, adjoint, section_first, section_second, jacobian, pattern, counts, courant, seam_codes):
    own, levels, rows, cells = adjoint.shape
    species = jacobian.shape[2]
    quads = levels * rows
    spec = lax.axis_size("spec")
    bf16, f32 = jnp.bfloat16, jnp.float32
    shape = jax.ShapeDtypeStruct
    here = lax.axis_index("tile") * spec + lax.axis_index("spec")
    scalars = lax.dynamic_slice_in_dim(jnp.asarray(table), here, 1, 0)
    cour = jnp.transpose(courant, (1, 0, 2))
    cores = [[0, 1], [2, 3]]
    opposite = [(i, i ^ 2) for i in range(spec)]

    start = call(
        start_body,
        shape((quads, own, cells), bf16),
        [whole(pl.ANY)],
        whole(VMEM),
        [VMEM((quads, own, cells), f32), pltpu.SemaphoreType.DMA((levels,))],
        (0, own * quads * cells * 6),
        "start",
    )(adjoint)
    opposite_start = lax.ppermute(start, "spec", opposite)
    near = lax.all_gather(start, "spec", axis_index_groups=cores)
    high, low = call(
        matrix_body,
        (shape((levels, species, species), bf16),) * 2,
        [whole(SMEM)] * 2 + [whole(VMEM)] * 3,
        (whole(VMEM),) * 2,
        [VMEM((levels, species, species), f32)],
        (14 * levels * species**3, 3 * levels * species**2 * 2),
        "matrix",
    )(pattern, scalars, section_first, section_second, jacobian)
    far = lax.all_gather(opposite_start, "spec", axis_index_groups=cores)
    half_rows = quads * own
    msg_rows = 2 * half_rows + 3 * quads
    msg = call(
        rim_body,
        shape((msg_rows, cells), bf16),
        [whole(SMEM)] * 2 + [whole(VMEM)] * 4,
        whole(VMEM),
        (),
        (2 * 2 * own * species * quads * cells, 4 * half_rows * cells * 2),
        "rim",
    )(counts, scalars, near, far, high, cour)
    got = lax.ppermute(msg, AXES, pairs)
    after = call(
        own_body,
        shape((quads, own, cells), f32),
        [whole(SMEM)] * 2 + [whole(pl.ANY)] + [whole(VMEM)] * 4,
        whole(VMEM),
        [VMEM((quads, own, cells), f32), pltpu.SemaphoreType.DMA((levels,))],
        (4 * own * species * quads * cells, 4 * half_rows * cells * 4),
        "own",
    )(counts, scalars, adjoint, near, far, high, low)
    core = lax.axis_index("spec") % 2
    onward = lax.dynamic_slice_in_dim(got, (1 - core) * half_rows, half_rows + 3 * quads, 0)
    handed = lax.all_gather(onward, "spec", axis_index_groups=cores)
    return call(
        end_body,
        shape((own, levels, rows, cells), f32),
        [whole(SMEM)] * 2 + [whole(VMEM)] * 4,
        whole(pl.ANY),
        [
            VMEM((9 * rows, levels, cells), f32),
            VMEM((quads, own, cells), f32),
            pltpu.SemaphoreType.DMA((levels,)),
        ],
        (20 * half_rows * cells, half_rows * cells * 12),
        "end",
    )(scalars, seam_codes, after, got, handed, cour)


def solution(mesh):
    in_specs = (
        P("spec", None, "tile", None),
        P("tile", None, None, None),
        P("tile", None, None, None),
        P("tile", None, None, None),
        P("tile", None, None, None),
        P("tile", None),
        P(None, "tile", None),
        P("tile", None),
    )
    table, pairs = partner_table(mesh.shape["tile"], mesh.shape["spec"])
    return jax.shard_map(
        functools.partial(shards, pairs, table),
        mesh=mesh,
        in_specs=in_specs,
        out_specs=P("spec", None, "tile", None),
        check_vma=False,
    )
```

```python
import functools

import jax
import jax.numpy as jnp
from jax import lax
from jax.experimental import pallas as pl
from jax.experimental.pallas import tpu as pltpu
from jax.sharding import PartitionSpec as P

NSUB = 4
section_weights = (0.4, 0.3, 0.2, 0.1)
coupling = 0.5
AXES = ("tile", "spec")
RUN = 4

GRANT = 8 << 20
VMEM = pltpu.VMEM
SMEM = pltpu.SMEM


def whole(space):
    return pl.BlockSpec(memory_space=space)


def call(body, out_shape, in_specs, out_specs, scratch=(), cost=(0, 0), name=None):
    return pl.pallas_call(
        body,
        out_shape=out_shape,
        in_specs=in_specs,
        out_specs=out_specs,
        scratch_shapes=list(scratch),
        cost_estimate=pl.CostEstimate(flops=cost[0], bytes_accessed=cost[1], transcendentals=0),
        compiler_params=pltpu.CompilerParams(vmem_limit_bytes=GRANT),
        name=name,
    )


def position():
    tile, spec = lax.axis_index("tile"), lax.axis_index("spec")
    core, half = spec % 2, spec // 2
    up = (tile + core + 1) % 2
    at = tile % RUN
    wraps = jnp.where(jnp.where(up == 1, at == RUN - 1, at == 0), 1, 0)
    return core, half, half + wraps - 2 * half * wraps, up == 1


def partners(tiles, spec):
    partner = []
    for tile in range(tiles):
        for s in range(spec):
            core = s % 2
            half = s // 2
            up = (tile % 2 == 0) == (core == 0)
            step = 1 if up else -1
            other = (tile + step) % tiles
            wraps = not 0 <= tile % RUN + step < RUN
            other_half = half ^ 1 if wraps else half
            partner.append(other * spec + other_half * 2 + core)
    for source, target in enumerate(partner):
        assert partner[target] == source
    return list(enumerate(partner))


def start_body(adj_ref, start_ref, held, sems):
    levels, rows = adj_ref.shape[1], adj_ref.shape[2]
    copies = []
    for level in range(levels):
        for row in range(rows):
            q = level * rows + row
            copies.append(
                pltpu.make_async_copy(adj_ref.at[:, level, row, :], held.at[q], sems.at[level])
            )
            copies[-1].start()
    for level in range(levels):
        for row in range(rows):
            copies[level * rows + row].wait()
        part = pl.ds(level * rows, rows)
        start_ref[part] = held[part].astype(jnp.bfloat16)


def matrix_body(pattern_ref, first_ref, second_ref, jac_ref, high_ref, low_ref, held):
    levels, size = first_ref.shape[1], first_ref.shape[2]
    block = size // 2
    w = section_weights
    ones = (w[0] + w[1] + w[2] + w[3], coupling * (w[1] + w[2] + w[3]))
    c2 = coupling * ones[1] - coupling * coupling * w[1]
    c3 = coupling**3 * w[3]
    lane = lax.broadcasted_iota(jnp.int32, (block, size), 1)
    row_id = lax.broadcasted_iota(jnp.int32, (size, size), 0)
    col_id = lax.broadcasted_iota(jnp.int32, (size, size), 1)
    diag = row_id == col_id

    def dot(a, b):
        return jnp.dot(a, b, preferred_element_type=jnp.float32)

    def used(level):
        parts = []
        for b in range(2):
            keep = jnp.where(lane < block, pattern_ref[0, level, b, 0], pattern_ref[0, level, b, 1])
            piece = jac_ref[0, level, pl.ds(b * block, block), :].astype(jnp.float32)
            parts.append(jnp.where(keep == 1, piece, 0.0).astype(jnp.bfloat16))
        return jnp.concatenate(parts, axis=0)

    for group in range(0, levels, 4):
        span = range(group, group + 4)
        t = [dot(second_ref[0, l], used(l)) for l in span]
        t_high = [x.astype(jnp.bfloat16) for x in t]
        t_low = [(x - h.astype(jnp.float32)).astype(jnp.bfloat16) for x, h in zip(t, t_high)]
        k = [
            dot(first_ref[0, l], h) + dot(first_ref[0, l], lo) for l, h, lo in zip(span, t_high, t_low)
        ]
        kb = [x.astype(jnp.bfloat16) for x in k]
        acc = [c3 * x + jnp.where(diag, c2, 0.0) for x in k]
        acc = [dot(a, x.astype(jnp.bfloat16)) + jnp.where(diag, ones[1], 0.0) for a, x in zip(kb, acc)]
        acc = [dot(a, x.astype(jnp.bfloat16)) for a, x in zip(kb, acc)]
        d = [
            x * ones[0] + dot(a, h.astype(jnp.bfloat16)) for x, a, h in zip(k, kb, acc)
        ]
        for i, l in enumerate(span):
            held[l] = d[i]
    half = position()[1]
    own = pl.multiple_of(half * block, block)
    far = pl.multiple_of((1 - half) * block, block)
    for l in range(levels):
        ordered = jnp.concatenate([held[l, pl.ds(own, block), :], held[l, pl.ds(far, block), :]], axis=0)
        turned = ordered.T
        high = turned.astype(jnp.bfloat16)
        high_ref[l] = high
        low_ref[l] = (turned - high.astype(jnp.float32)).astype(jnp.bfloat16)


def fields(near_ref, far_ref, level, rows):
    return jnp.concatenate(
        [
            jnp.concatenate([near_ref[0, q], near_ref[1, q], far_ref[0, q], far_ref[1, q]], axis=0)
            for q in range(level * rows, level * rows + rows)
        ],
        axis=1,
    )


def rim_body(counts_ref, near_ref, far_ref, high_ref, cour_ref, msg_ref):
    rows = cour_ref.shape[0]
    levels = high_ref.shape[0]
    cells = near_ref.shape[3]
    own = near_ref.shape[2]
    quads = levels * rows
    _, half, other_half, _ = position()
    aim = pl.multiple_of(other_half * 2 * own, 2 * own)
    near_aim = other_half == half
    lane = lax.broadcasted_iota(jnp.int32, (own, cells), 1)
    sections = (0, quads * own + 3 * quads)
    for level in range(levels):
        x = fields(near_ref, far_ref, level, rows)
        chem = jnp.dot(high_ref[level, pl.ds(aim, 2 * own), :], x, preferred_element_type=jnp.float32)
        for row in range(rows):
            q = level * rows + row
            active = lane < counts_ref[0, level] - row * cells
            for core in range(2):
                base = jnp.where(
                    near_aim,
                    near_ref[core, q].astype(jnp.float32),
                    far_ref[core, q].astype(jnp.float32),
                )
                term = chem[core * own : (core + 1) * own, row * cells : (row + 1) * cells]
                value = base + jnp.where(active, term, 0.0)
                msg_ref[pl.ds(sections[core] + q * own, own), :] = value.astype(jnp.bfloat16)
    cour = jnp.concatenate([cour_ref[row] for row in range(rows)], axis=0)
    first = quads * own
    for piece in range(3):
        part = cour.astype(jnp.bfloat16)
        msg_ref[pl.ds(first + piece * quads, quads), :] = part
        cour = cour - part.astype(jnp.float32)


def own_body(counts_ref, adj_ref, near_ref, far_ref, high_ref, low_ref, after_ref, held, sems):
    levels, rows = adj_ref.shape[1], adj_ref.shape[2]
    own, cells = adj_ref.shape[0], adj_ref.shape[3]
    copies = []
    for level in range(levels):
        for row in range(rows):
            q = level * rows + row
            copies.append(
                pltpu.make_async_copy(adj_ref.at[:, level, row, :], held.at[q], sems.at[level])
            )
            copies[-1].start()
    mine = pl.multiple_of(lax.axis_index("spec") * own, own)
    lane = lax.broadcasted_iota(jnp.int32, (own, cells), 1)
    for level in range(levels):
        x = fields(near_ref, far_ref, level, rows)
        both = jnp.concatenate(
            [high_ref[level, pl.ds(mine, own), :], low_ref[level, pl.ds(mine, own), :]], axis=0
        )
        chem = jnp.dot(both, x, preferred_element_type=jnp.float32)
        chem = chem[:own] + chem[own:]
        for row in range(rows):
            copies[level * rows + row].wait()
        for row in range(rows):
            q = level * rows + row
            active = lane < counts_ref[0, level] - row * cells
            term = chem[:, row * cells : (row + 1) * cells]
            after_ref[q] = held[q] + jnp.where(active, term, 0.0)


def taps(rise, fall, rows):
    table = []
    for i in range(rows, 2 * rows):
        weight = {i: None}
        for _ in range(NSUB):
            fresh = {}

            def add(j, value, fresh=fresh):
                fresh[j] = value if j not in fresh else fresh[j] + value

            for j, value in weight.items():
                keep = 1.0 - rise[j] + fall[j]
                add(j, keep if value is None else value * keep)
                add(j + 1, rise[j] if value is None else value * rise[j])
                add(j - 1, -fall[j] if value is None else -(value * fall[j]))
            weight = fresh
        table.append(weight)
    return table


def end_body(codes_ref, after_ref, got_ref, handed_ref, cour_ref, out_ref, coef, built, sems):
    rows = cour_ref.shape[0]
    levels = cour_ref.shape[1]
    own, cells = after_ref.shape[1], after_ref.shape[2]
    quads = levels * rows
    body_rows = quads * own
    cour_rows = 3 * quads
    core, _, _, up = position()
    got_at = core * (body_rows + cour_rows)
    handed_at = core * cour_rows
    handed_cour = (1 - core) * body_rows
    one = jnp.ones((cells, cells), jnp.float32)
    r = lax.broadcasted_iota(jnp.int32, (cells, cells), 0)
    c = lax.broadcasted_iota(jnp.int32, (cells, cells), 1)

    def turn(code):
        return jnp.where(jnp.where(code == 1, cells - 1 - c, c) == r, one, 0.0).astype(jnp.bfloat16)

    turn_up, turn_down = turn(codes_ref[0, 0]), turn(codes_ref[0, 1])

    def pair(got_row, handed_row, count):
        a = got_ref[pl.ds(pl.multiple_of(got_row, 32), count), :]
        b = handed_ref[1 - core, pl.ds(pl.multiple_of(handed_row, 32), count), :]
        a32, b32 = a.astype(jnp.float32), b.astype(jnp.float32)
        above = jnp.where(up, a32, b32).astype(jnp.bfloat16)
        below = jnp.where(up, b32, a32).astype(jnp.bfloat16)
        return (
            jnp.dot(above, turn_up, preferred_element_type=jnp.float32),
            jnp.dot(below, turn_down, preferred_element_type=jnp.float32),
        )

    pieces = pair(body_rows, handed_cour, cour_rows)
    above_cour, below_cour = [x[:quads] + x[quads : 2 * quads] + x[2 * quads :] for x in pieces]
    stack = [below_cour[i * levels : (i + 1) * levels] for i in range(rows)]
    stack += [cour_ref[i] for i in range(rows)]
    stack += [above_cour[i * levels : (i + 1) * levels] for i in range(rows)]
    rise = [jnp.maximum(x, 0.0) for x in stack]
    fall = [None] + [jnp.minimum(x, 0.0) for x in stack[:-1]]
    table = taps(rise, fall, rows)
    slot = {}
    for i, weight in enumerate(table):
        for j in sorted(weight):
            slot[i, j] = len(slot)
            coef[slot[i, j]] = weight[j]
    copies = []
    for level in range(levels):
        q = level * rows
        above, below = pair(got_at + q * own, handed_at + q * own, rows * own)
        stack = [below[i * own : (i + 1) * own] for i in range(rows)]
        stack += [after_ref[q + i] for i in range(rows)]
        stack += [above[i * own : (i + 1) * own] for i in range(rows)]
        for i in range(rows):
            total = None
            for j in sorted(table[i]):
                term = coef[slot[i, j], pl.ds(level, 1), :] * stack[j]
                total = term if total is None else total + term
            built[q + i] = total
        for i in range(rows):
            copies.append(
                pltpu.make_async_copy(built.at[q + i], out_ref.at[:, level, i, :], sems.at[level])
            )
            copies[-1].start()
    for copy in copies:
        copy.wait()


def shards(pairs, adjoint, section_first, section_second, jacobian, pattern, counts, courant, seam_codes):
    own, levels, rows, cells = adjoint.shape
    species = jacobian.shape[2]
    quads = levels * rows
    spec = lax.axis_size("spec")
    bf16, f32 = jnp.bfloat16, jnp.float32
    shape = jax.ShapeDtypeStruct
    cour = jnp.transpose(courant, (1, 0, 2))
    cores = [[0, 1], [2, 3]]
    opposite = [(i, i ^ 2) for i in range(spec)]

    start = call(
        start_body,
        shape((quads, own, cells), bf16),
        [whole(pltpu.HBM)],
        whole(VMEM),
        [VMEM((quads, own, cells), f32), pltpu.SemaphoreType.DMA((levels,))],
        (0, own * quads * cells * 6),
        "start",
    )(adjoint)
    opposite_start = lax.ppermute(start, "spec", opposite)
    near = lax.all_gather(start, "spec", axis_index_groups=cores)
    high, low = call(
        matrix_body,
        (shape((levels, species, species), bf16),) * 2,
        [whole(SMEM)] + [whole(VMEM)] * 3,
        (whole(VMEM),) * 2,
        [VMEM((levels, species, species), f32)],
        (14 * levels * species**3, 3 * levels * species**2 * 2),
        "matrix",
    )(pattern, section_first, section_second, jacobian)
    far = lax.all_gather(opposite_start, "spec", axis_index_groups=cores)
    half_rows = quads * own
    msg_rows = 2 * half_rows + 3 * quads
    msg = call(
        rim_body,
        shape((msg_rows, cells), bf16),
        [whole(SMEM)] + [whole(VMEM)] * 4,
        whole(VMEM),
        (),
        (2 * 2 * own * species * quads * cells, 4 * half_rows * cells * 2),
        "rim",
    )(counts, near, far, high, cour)
    got = lax.ppermute(msg, AXES, pairs)
    after = call(
        own_body,
        shape((quads, own, cells), f32),
        [whole(SMEM)] + [whole(pltpu.HBM)] + [whole(VMEM)] * 4,
        whole(VMEM),
        [VMEM((quads, own, cells), f32), pltpu.SemaphoreType.DMA((levels,))],
        (4 * own * species * quads * cells, 4 * half_rows * cells * 4),
        "own",
    )(counts, adjoint, near, far, high, low)
    core = lax.axis_index("spec") % 2
    onward = lax.dynamic_slice_in_dim(got, (1 - core) * half_rows, half_rows + 3 * quads, 0)
    handed = lax.all_gather(onward, "spec", axis_index_groups=cores)
    return call(
        end_body,
        shape((own, levels, rows, cells), f32),
        [whole(SMEM)] + [whole(VMEM)] * 4,
        whole(pltpu.HBM),
        [
            VMEM((9 * rows, levels, cells), f32),
            VMEM((quads, own, cells), f32),
            pltpu.SemaphoreType.DMA((levels,)),
        ],
        (20 * half_rows * cells, half_rows * cells * 12),
        "end",
    )(seam_codes, after, got, handed, cour)


def solution(mesh):
    in_specs = (
        P("spec", None, "tile", None),
        P("tile", None, None, None),
        P("tile", None, None, None),
        P("tile", None, None, None),
        P("tile", None, None, None),
        P("tile", None),
        P(None, "tile", None),
        P("tile", None),
    )
    pairs = partners(mesh.shape["tile"], mesh.shape["spec"])
    return jax.shard_map(
        functools.partial(shards, pairs),
        mesh=mesh,
        in_specs=in_specs,
        out_specs=P("spec", None, "tile", None),
        check_vma=False,
    )
```
